32 devices in a mesh: leaf: 8 (over z, y), rows: 4 (over x, core).
Axes of the slice: x: 2, y: 2, z: 4, core: 2. Of those that a mesh axis runs over, the one named last changes fastest.
Arguments:
- sigma_top: float32 [2048, 1024], P('leaf'), may hold values from -4 to 40, as said below
- panel_top: float32 [1024, 12288], P(None, 'leaf'), may hold values from -0.125 to 0.125
- diag_top: float32 [12288, 256], P('leaf'), may hold values from -4 to 20, as said below
- panel_mid: float32 [1024, 24576], P(None, ('leaf', 'rows')), may hold values from -0.125 to 0.125
- diag_mid: float32 [24576, 256], P(('leaf', 'rows')), may hold values from -4 to 20, as said below
- pattern_mid: int32 [4, 4], replicated, may hold values from 0 to 23, as said below
- panel_low: float32 [1024, 49152], P(None, ('leaf', 'rows')), may hold values from -0.125 to 0.125
- diag_low: float32 [49152, 256], P(('leaf', 'rows')), may hold values from -4 to 20, as said below
- pattern_low: int32 [8, 4], replicated, may hold values from 0 to 23, as said below
Outputs:
- cross_top: float32 [1024, 12288], P('rows', 'leaf')
- marginal_top: float32 [12288, 256], P(('leaf', 'rows'))
- cross_mid: float32 [1024, 24576], P(None, ('leaf', 'rows'))
- marginal_mid: float32 [24576, 256], P(('leaf', 'rows'))
- cross_low: float32 [1024, 49152], P(None, ('leaf', 'rows'))
- marginal_low: float32 [49152, 256], P(('leaf', 'rows'))
The draws below stay inside these ranges and needn't reach their ends.
Inputs may be any that keep to these rules, and one draw needn't show every extreme that they name: Each block of 1024 rows of sigma_top is symmetric. `diag_top`: each 256 x 256 block is symmetric. `diag_mid`: each block of 256 rows is symmetric. `diag_low`: each block of 256 rows is symmetric. `pattern_mid`: the 4 entries of a row are different; rows 2i and 2i + 1 together name 8 different blocks. `pattern_low`: the 4 entries of a row are different; rows 2i and 2i + 1 together name 8 different blocks.
All inputs are finite; a program needn't handle non-finite values.
Results may differ from the reference program's by a relative error of at most 0.00009.
Values sent between devices are 32-bit elements; how exact they have to be, the bound alone decides.
A program may use at most 192 MiB of HBM per device.

```python
import math
import jax
import jax.numpy as jnp
from jax import lax

BLOCK = 256
NBLOCK = 24
STRUCT_BLOCKS = 4
ORDER = 6144
STRUCT = 1024
NTOP = 2
NMID = 4
NLOW = 8


def symmetric_blocks(key, block_count, block_side, base_low, base_high, off_scale):
    key_rough, key_levels = jax.random.split(key, 2)
    rough_part = jax.random.normal(key_rough, (block_count, block_side, block_side), jnp.float32)
    mixed_part = (rough_part + jnp.swapaxes(rough_part, 1, 2)) * (off_scale / math.sqrt(2.0 * block_side))
    levels = jnp.exp(jax.random.uniform(key_levels, (block_count, block_side), jnp.float32, math.log(base_low), math.log(base_high)))
    eye_table = jnp.eye(block_side, dtype=jnp.float32)
    whole_set = mixed_part + eye_table[None, :, :] * levels[:, :, None]
    return whole_set


def pattern_rows(key, row_total):
    order_perm = jax.random.permutation(key, NBLOCK).astype(jnp.int32)
    spots = (jnp.arange(row_total * STRUCT_BLOCKS, dtype=jnp.int32) % NBLOCK).reshape(row_total, STRUCT_BLOCKS)
    return order_perm[spots]


def draw_sigma_top(key, part):
    return symmetric_blocks(jax.random.fold_in(key, 11), NTOP, STRUCT, 1.0, 4.0, 0.45).reshape(NTOP * STRUCT, STRUCT)


def draw_diag_top(key, part):
    return symmetric_blocks(jax.random.fold_in(key, 12), NTOP * NBLOCK, BLOCK, 0.5, 2.0, 0.3).reshape(NTOP * ORDER, BLOCK)


def draw_diag_mid(key, part):
    return symmetric_blocks(jax.random.fold_in(key, 13), NMID * NBLOCK, BLOCK, 0.5, 2.0, 0.3).reshape(NMID * ORDER, BLOCK)


def draw_diag_low(key, part):
    return symmetric_blocks(jax.random.fold_in(key, 14), NLOW * NBLOCK, BLOCK, 0.5, 2.0, 0.3).reshape(NLOW * ORDER, BLOCK)


def draw_pattern_mid(key, part):
    return pattern_rows(jax.random.fold_in(key, 15), NMID)


def draw_pattern_low(key, part):
    return pattern_rows(jax.random.fold_in(key, 16), NLOW)


def level_of(stream_key, shape, cuts, low, top_value):
    loudness = 1.0
    for position, parts in cuts:
        heights = jax.random.uniform(jax.random.fold_in(jax.random.fold_in(stream_key, 6), position), (parts,), jnp.float32, low / len(cuts), top_value / len(cuts))
        loudness = loudness * jnp.repeat(jnp.exp(heights), shape[position] // parts).reshape((-1,) + (1,) * (len(shape) - 1 - position))
    return loudness


def gaussian(own_key, extent, scale, reach, shards=(), kind=jnp.bfloat16):
    level = level_of(own_key, extent, shards, -0.22, 0.18) if shards else 1.0
    drawn = jax.random.normal(own_key, extent, jnp.float32) * scale * level
    return jnp.minimum(jnp.maximum(drawn, -reach), reach).astype(kind)


def setup_inputs(seed: int = 0) -> dict:
    seeds = jax.random.split(jax.random.key(seed), 10)
    return {
        "sigma_top": draw_sigma_top(jax.random.fold_in(seeds[9], 71), 0),
        "panel_top": gaussian(seeds[1], (STRUCT, NTOP * ORDER), (2 * STRUCT) ** -0.5, 0.125, ((1, 8),), jnp.float32),
        "diag_top": draw_diag_top(jax.random.fold_in(seeds[9], 71), 0),
        "panel_mid": gaussian(seeds[3], (STRUCT, NMID * ORDER), (2 * STRUCT) ** -0.5, 0.125, ((1, 32),), jnp.float32),
        "diag_mid": draw_diag_mid(jax.random.fold_in(seeds[9], 71), 0),
        "pattern_mid": draw_pattern_mid(jax.random.fold_in(seeds[9], 71), 0),
        "panel_low": gaussian(seeds[6], (STRUCT, NLOW * ORDER), (2 * STRUCT) ** -0.5, 0.125, ((1, 32),), jnp.float32),
        "diag_low": draw_diag_low(jax.random.fold_in(seeds[9], 71), 0),
        "pattern_low": draw_pattern_low(jax.random.fold_in(seeds[9], 71), 0),
    }


HIGH = lax.Precision.HIGHEST


def block_diagonal(blocks):
    block_count = blocks.shape[0]
    block_side = blocks.shape[1]
    eye_table = jnp.eye(block_count, dtype=blocks.dtype)
    spread_out = blocks[:, :, None, :] * eye_table[:, None, :, None]
    return spread_out.reshape(block_count * block_side, block_count * block_side)


def level_panel(inputs):
    covariance, panel_cols, diag_blocks = inputs
    cover_cols = -jnp.dot(covariance, panel_cols, precision=HIGH, preferred_element_type=jnp.float32)
    terms = jnp.einsum("sai,saj->aij", panel_cols.reshape(STRUCT, NBLOCK, BLOCK), cover_cols.reshape(STRUCT, NBLOCK, BLOCK), precision=HIGH)
    return cover_cols, diag_blocks - terms.reshape(NBLOCK * BLOCK, BLOCK)


def child_cov(inputs):
    parent_cov, parent_panel, parent_diag, wanted = inputs
    chosen = jnp.take(parent_panel.reshape(STRUCT, NBLOCK, BLOCK), wanted, axis=1).reshape(STRUCT, STRUCT_BLOCKS * BLOCK)
    chosen_diag = jnp.take(parent_diag.reshape(NBLOCK, BLOCK, BLOCK), wanted, axis=0)
    product = jnp.dot(parent_cov, chosen, precision=HIGH, preferred_element_type=jnp.float32)
    return jnp.dot(chosen.T, product, precision=HIGH, preferred_element_type=jnp.float32) + block_diagonal(chosen_diag)


def flat_cover(cover_stack):
    return jnp.transpose(cover_stack, (1, 0, 2)).reshape(STRUCT, -1)


def reference(sigma_top, panel_top, diag_top, panel_mid, diag_mid, pattern_mid, panel_low, diag_low, pattern_low):
    top_count = sigma_top.shape[0] // STRUCT
    mid_count = pattern_mid.shape[0]
    low_count = pattern_low.shape[0]
    top_cov = sigma_top.reshape(top_count, STRUCT, STRUCT)
    top_panel = jnp.transpose(panel_top.reshape(STRUCT, top_count, ORDER), (1, 0, 2))
    top_diag = diag_top.reshape(top_count, ORDER, BLOCK)
    top_cover, top_marg = lax.map(level_panel, (top_cov, top_panel, top_diag))
    parent_mid = jnp.arange(mid_count, dtype=jnp.int32) // 2
    mid_cov = lax.map(child_cov, (top_cov[parent_mid], top_panel[parent_mid], top_diag[parent_mid], pattern_mid))
    mid_panel = jnp.transpose(panel_mid.reshape(STRUCT, mid_count, ORDER), (1, 0, 2))
    mid_diag = diag_mid.reshape(mid_count, ORDER, BLOCK)
    mid_cover, mid_marg = lax.map(level_panel, (mid_cov, mid_panel, mid_diag))
    parent_low = jnp.arange(low_count, dtype=jnp.int32) // 2
    low_cov = lax.map(child_cov, (mid_cov[parent_low], mid_panel[parent_low], mid_diag[parent_low], pattern_low))
    low_panel = jnp.transpose(panel_low.reshape(STRUCT, low_count, ORDER), (1, 0, 2))
    low_diag = diag_low.reshape(low_count, ORDER, BLOCK)
    low_cover, low_marg = lax.map(level_panel, (low_cov, low_panel, low_diag))
    return (flat_cover(top_cover), top_marg.reshape(-1, BLOCK), flat_cover(mid_cover), mid_marg.reshape(-1, BLOCK), flat_cover(low_cover), low_marg.reshape(-1, BLOCK))
```

```python
import functools

import jax
import jax.numpy as jnp
from jax import lax
from jax.experimental import pallas as pl
from jax.experimental.pallas import tpu as pltpu
from jax.sharding import PartitionSpec as P

HIGH = lax.Precision.HIGH
F32 = jnp.float32
BF16 = jnp.bfloat16
VMEM_LIMIT = 56 * 1024 * 1024


def swap(value, axis, distance):
    return lax.ppermute(value, axis, [(i, i ^ distance) for i in range(lax.axis_size(axis))])


def split(value):
    high = value.astype(BF16)
    return high, (value - high.astype(F32)).astype(BF16)


def dot3(left, right, dims):
    dot = functools.partial(
        lax.dot_general, dimension_numbers=(dims, ((), ())), preferred_element_type=F32
    )
    return dot(left[0], right[0]) + (dot(left[0], right[1]) + dot(left[1], right[0]))


NN = ((1,), (0,))
TN = ((0,), (0,))


def params():
    return pltpu.CompilerParams(
        dimension_semantics=("arbitrary",), vmem_limit_bytes=VMEM_LIMIT
    )


def select_kernel(slots, count, piece, table, panel_ref, diag_ref, *outs):
    slot = pl.program_id(0)
    block = diag_ref.shape[1]

    @pl.when(slot < slots)
    def _():
        owned = table[slots + slot] > 0
        for i in range(count):
            start = pl.multiple_of(table[2 * slots + i] * piece, 8)
            outs[i][...] = jnp.where(owned, panel_ref[pl.ds(start, piece), :], 0.0)

    @pl.when(slot == slots)
    def _():
        for i in range(count):
            which = table[2 * slots + count + i]
            start = pl.multiple_of(table[which] * block, 8)
            owned = table[slots + which] > 0
            outs[i][...] = jnp.where(owned, diag_ref[pl.ds(start, piece), :], 0.0)


def select(panel, diag, wanted, owned, within, quarters, row_block, rows_block, piece):
    slots = wanted.shape[0]
    count = len(quarters)
    block = diag.shape[1]
    table = jnp.concatenate(
        [
            wanted,
            owned.astype(jnp.int32),
            jnp.stack(within).astype(jnp.int32),
            jnp.stack(quarters).astype(jnp.int32),
            jnp.reshape(row_block, (1,)).astype(jnp.int32),
        ]
    )
    last = 2 * slots + 2 * count
    return pl.pallas_call(
        functools.partial(select_kernel, slots, count, piece),
        grid_spec=pltpu.PrefetchScalarGridSpec(
            num_scalar_prefetch=1,
            grid=(slots + 1,),
            in_specs=[
                pl.BlockSpec(
                    (rows_block, block),
                    lambda s, t: (t[last], t[jnp.minimum(s, slots - 1)]),
                ),
                pl.BlockSpec(diag.shape, lambda s, t: (0, 0)),
            ],
            out_specs=[pl.BlockSpec((piece, block), lambda s, t: (0, s))] * count,
        ),
        out_shape=[jax.ShapeDtypeStruct((piece, (slots + 1) * block), F32)] * count,
        compiler_params=params(),
        cost_estimate=pl.CostEstimate(
            flops=0, transcendentals=0, bytes_accessed=8 * count * piece * (slots + 1) * block
        ),
        name="select",
    )(table, panel, diag)


def assemble_kernel(leaf_parts, row_parts, piece, table, own_ref, *rest):
    parts, out_ref = rest[:-1], rest[-1]
    place, row = table[0], table[1]
    own_rows = own_ref.shape[0]
    out_ref[pl.ds(pl.multiple_of(place * own_rows, 8), own_rows), :] = own_ref[...]
    for k in range(row_parts):
        for d in range(1, leaf_parts):
            start = pl.multiple_of((place ^ d) * own_rows + (row ^ k) * piece, 8)
            out_ref[pl.ds(start, piece), :] = parts[k][pl.ds((d - 1) * piece, piece), :]


def assemble(own, parts, place, row):
    piece = own.shape[0] // len(parts)
    leaf_parts = own.shape[1] // own.shape[0]
    vmem = pl.BlockSpec(memory_space=pltpu.VMEM)
    return pl.pallas_call(
        functools.partial(assemble_kernel, leaf_parts, len(parts), piece),
        in_specs=[pl.BlockSpec(memory_space=pltpu.SMEM)] + [vmem] * (1 + len(parts)),
        out_specs=vmem,
        out_shape=jax.ShapeDtypeStruct((own.shape[1], own.shape[1]), F32),
        compiler_params=pltpu.CompilerParams(vmem_limit_bytes=VMEM_LIMIT),
        cost_estimate=pl.CostEstimate(
            flops=0, transcendentals=0, bytes_accessed=8 * own.shape[1] ** 2
        ),
        name="assemble",
    )(jnp.stack([place, row]).astype(jnp.int32), own, *parts)


def child_kernel(row_parts, table, cov_ref, *rest):
    parts = rest[:row_parts]
    out_ref, cov_h, cov_l, sel_h, sel_l, diag_s, mid_h, mid_l = rest[row_parts:]
    step = pl.program_id(0)
    row = table[0]
    piece = parts[0].shape[0]
    width = out_ref.shape[1]
    order = cov_ref.shape[0]

    @pl.when(step == 0)
    def _():
        for k in range(row_parts):
            at = pl.ds(pl.multiple_of((row ^ k) * piece, 16), piece)
            sel_h[at, :], sel_l[at, :] = split(parts[k][:, :order])
            diag_s[at, :] = parts[k][:, order:]
            own = pl.ds(k * piece, piece)
            cov_h[own, :], cov_l[own, :] = split(cov_ref[own, :])

    cols = pl.ds(pl.multiple_of(step * width, 128), width)
    chosen = (sel_h[:, cols], sel_l[:, cols])
    for k in range(row_parts):
        at = pl.ds(k * piece, piece)
        mid_h[at, :], mid_l[at, :] = split(dot3((cov_h[at, :], cov_l[at, :]), chosen, NN))
    product = (mid_h[...], mid_l[...])
    for k in range(order // width):
        at = pl.ds(k * width, width)
        out_ref[at, :] = dot3((sel_h[:, at], sel_l[:, at]), product, TN)
    out_ref[cols, :] += diag_s[cols, :]


def child_cov(cov, parts, row):
    order = cov.shape[0]
    row_parts = len(parts)
    block = parts[0].shape[1] - order
    whole = lambda shape: pl.BlockSpec(
        shape, lambda s, t: (0, 0), pipeline_mode=pl.Buffered(1)
    )
    return pl.pallas_call(
        functools.partial(child_kernel, row_parts),
        grid_spec=pltpu.PrefetchScalarGridSpec(
            num_scalar_prefetch=1,
            grid=(order // block,),
            in_specs=[whole(cov.shape)] + [whole(parts[0].shape)] * row_parts,
            out_specs=pl.BlockSpec((order, block), lambda s, t: (0, s)),
            scratch_shapes=[pltpu.VMEM((order, order), BF16)] * 4
            + [pltpu.VMEM((order, block), F32)]
            + [pltpu.VMEM((order, block), BF16)] * 2,
        ),
        out_shape=jax.ShapeDtypeStruct((order, order), F32),
        compiler_params=params(),
        cost_estimate=pl.CostEstimate(
            flops=12 * order**3, transcendentals=0, bytes_accessed=12 * order**2
        ),
        name="child_cov",
    )(jnp.reshape(row, (1,)).astype(jnp.int32), cov, *parts)


def panel_kernel(cov_ref, panel_ref, diag_ref, cross_ref, marg_ref, cov_h, cov_l):
    order = cov_ref.shape[0]
    block = panel_ref.shape[1]

    @pl.when(pl.program_id(0) == 0)
    def _():
        for k in range(order // block):
            at = pl.ds(k * block, block)
            cov_h[at, :], cov_l[at, :] = split(cov_ref[at, :])

    cols = split(panel_ref[...])
    total = diag_ref[...]
    for k in range(order // block):
        at = pl.ds(k * block, block)
        part = -dot3((cov_h[at, :], cov_l[at, :]), cols, NN)
        cross_ref[at, :] = part
        own = slice(k * block, (k + 1) * block)
        total = total - dot3((cols[0][own], cols[1][own]), split(part), TN)
    marg_ref[...] = total


def level_panel(cov, panel, diag):
    order = cov.shape[0]
    block = diag.shape[1]
    count = panel.shape[1] // block
    return pl.pallas_call(
        panel_kernel,
        grid=(count,),
        in_specs=[
            pl.BlockSpec(cov.shape, lambda a: (0, 0), pipeline_mode=pl.Buffered(1)),
            pl.BlockSpec((order, block), lambda a: (0, a)),
            pl.BlockSpec((block, block), lambda a: (a, 0)),
        ],
        out_specs=[
            pl.BlockSpec((order, block), lambda a: (0, a)),
            pl.BlockSpec((block, block), lambda a: (a, 0)),
        ],
        out_shape=[
            jax.ShapeDtypeStruct(panel.shape, F32),
            jax.ShapeDtypeStruct(diag.shape, F32),
        ],
        scratch_shapes=[pltpu.VMEM((order, order), BF16)] * 2,
        compiler_params=params(),
        cost_estimate=pl.CostEstimate(
            flops=6 * panel.shape[1] * order * (order + block),
            transcendentals=0,
            bytes_accessed=4 * order * (order + 2 * panel.shape[1]),
        ),
        name="level_panel",
    )(cov, panel, diag)


def ownership(wanted, local_count, place):
    return wanted % local_count, wanted // local_count == place


def over_rows(mine):
    across = swap(mine, "rows", 2)
    return [mine, swap(mine, "rows", 1), across, swap(across, "rows", 1)]


def local(
    sigma_top,
    panel_top,
    diag_top,
    panel_mid,
    diag_mid,
    pattern_mid,
    panel_low,
    diag_low,
    pattern_low,
):
    block = diag_top.shape[1]
    struct_rows = panel_top.shape[0]
    row_count = lax.axis_size("rows")
    leaf = lax.axis_index("leaf")
    row = lax.axis_index("rows")
    piece = struct_rows // row_count
    quad_place = leaf % 4
    quad_number = leaf // 4
    middle = leaf // 2
    mid_bit = middle % 2
    low_bit = leaf % 2

    top_local = panel_top.shape[1] // block

    def top_part(child):
        wanted, owned = ownership(pattern_mid[child], top_local, quad_place)
        zero = jnp.zeros_like(row)
        return select(
            panel_top, diag_top, wanted, owned, [zero], [row], row, piece, piece
        )[0]

    other_top = top_part(2 * quad_number + 1 - mid_bit)
    own_top = top_part(middle)
    share = sigma_top.shape[0] // row_count
    sig = lax.dynamic_slice_in_dim(sigma_top, row * share, share, 0)
    sig_1 = swap(sig, "leaf", 1)
    sig_2 = swap(sig, "leaf", 2)
    sig_3 = swap(sig_1, "leaf", 2)
    own_top = own_top + swap(other_top, "leaf", 2)
    own_top = own_top + swap(own_top, "leaf", 1)
    sig_parts = over_rows(jnp.concatenate([sig_1, sig_2, sig_3], axis=0))
    top_parts = over_rows(own_top)

    mid_local = panel_mid.shape[1] // block
    places = [row ^ k for k in range(row_count)]

    def mid_part(child):
        wanted, owned = ownership(pattern_low[child], mid_local, low_bit * row_count + row)
        return select(
            panel_mid,
            diag_mid,
            wanted,
            owned,
            places,
            places,
            jnp.zeros_like(row),
            struct_rows,
            piece,
        )

    theirs = mid_part(2 * middle + 1 - low_bit)
    theirs_2 = theirs[2] + swap(theirs[3], "rows", 1)
    theirs_0 = theirs[0] + swap(theirs[1], "rows", 1)
    ours = mid_part(leaf)
    ours_2 = ours[2] + swap(ours[3], "rows", 1) + swap(theirs_2, "leaf", 1)
    ours_0 = ours[0] + swap(ours[1], "rows", 1) + swap(theirs_0, "leaf", 1)
    mid_parts = over_rows(ours_0 + swap(ours_2, "rows", 2))

    top_cov = assemble(sigma_top, sig_parts, quad_place, row)
    mid_cov = child_cov(top_cov, top_parts, row)
    cross_mid, marginal_mid = level_panel(mid_cov, panel_mid, diag_mid)

    dot = functools.partial(jnp.dot, precision=HIGH, preferred_element_type=F32)
    cov_rows = lax.dynamic_slice_in_dim(top_cov, row * piece, piece, 0)
    cross_top = -dot(cov_rows, panel_top)
    own_rows = diag_top.shape[0] // row_count
    chunk = block if own_rows % block == 0 else own_rows - own_rows // block * block
    own_cols = lax.dynamic_slice_in_dim(panel_top, row * own_rows, own_rows, 1)
    product = dot(top_cov, own_cols)
    terms = []
    for i in range(own_rows // chunk):
        start = (row * own_rows + i * chunk) // block * block
        cols = lax.dynamic_slice_in_dim(panel_top, start, block, 1)
        terms.append(dot(product[:, i * chunk : (i + 1) * chunk].T, cols))
    own_diag = lax.dynamic_slice_in_dim(diag_top, row * own_rows, own_rows, 0)
    marginal_top = own_diag + jnp.concatenate(terms, axis=0)

    low_cov = child_cov(mid_cov, mid_parts, row)
    cross_low, marginal_low = level_panel(low_cov, panel_low, diag_low)
    return (cross_top, marginal_top, cross_mid, marginal_mid, cross_low, marginal_low)


def solution(mesh):
    return jax.shard_map(
        local,
        mesh=mesh,
        in_specs=(
            P("leaf", None),
            P(None, "leaf"),
            P("leaf", None),
            P(None, ("leaf", "rows")),
            P(("leaf", "rows"), None),
            P(),
            P(None, ("leaf", "rows")),
            P(("leaf", "rows"), None),
            P(),
        ),
        out_specs=(
            P("rows", "leaf"),
            P(("leaf", "rows"), None),
            P(None, ("leaf", "rows")),
            P(("leaf", "rows"), None),
            P(None, ("leaf", "rows")),
            P(("leaf", "rows"), None),
        ),
        check_vma=False,
    )
```

```python
import functools

import jax
import jax.numpy as jnp
from jax import lax
from jax.experimental import pallas as pl
from jax.experimental.pallas import tpu as pltpu
from jax.sharding import PartitionSpec as P

HIGH = lax.Precision.HIGH
F32 = jnp.float32
BF16 = jnp.bfloat16
VMEM_LIMIT = 56 * 1024 * 1024
CHUNKS = 2


def swap(value, axis, distance):
    return lax.ppermute(value, axis, [(i, i ^ distance) for i in range(lax.axis_size(axis))])


def split(value):
    high = value.astype(BF16)
    return high, (value - high.astype(F32)).astype(BF16)


def dot3(left, right, dims):
    dot = functools.partial(
        lax.dot_general, dimension_numbers=(dims, ((), ())), preferred_element_type=F32
    )
    return dot(left[0], right[0]) + (dot(left[0], right[1]) + dot(left[1], right[0]))


NN = ((1,), (0,))
TN = ((0,), (0,))


def params():
    return pltpu.CompilerParams(
        dimension_semantics=("arbitrary",), vmem_limit_bytes=VMEM_LIMIT
    )


def select_kernel(slots, count, piece, table, panel_ref, diag_ref, *rest):
    outs = rest[-count * CHUNKS :]
    slot = pl.program_id(0)
    block = diag_ref.shape[1]
    part = piece // CHUNKS

    @pl.when(slot < slots)
    def _():
        owned = table[slots + slot] > 0
        for i in range(count):
            for u in range(CHUNKS):
                start = pl.multiple_of(table[2 * slots + i] * piece + u * part, 8)
                outs[i * CHUNKS + u][...] = jnp.where(owned, panel_ref[pl.ds(start, part), :], 0.0)

    @pl.when(slot == slots)
    def _():
        for i in range(count):
            which = table[2 * slots + count + i]
            owned = table[slots + which] > 0
            for u in range(CHUNKS):
                start = pl.multiple_of(table[which] * block + u * part, 8)
                outs[i * CHUNKS + u][...] = jnp.where(owned, diag_ref[pl.ds(start, part), :], 0.0)


def select(panel, diag, wanted, owned, within, quarters, row_block, rows_block, piece, after):
    slots = wanted.shape[0]
    count = len(quarters)
    block = diag.shape[1]
    table = jnp.concatenate(
        [
            wanted,
            owned.astype(jnp.int32),
            jnp.stack(within).astype(jnp.int32),
            jnp.stack(quarters).astype(jnp.int32),
            jnp.reshape(row_block, (1,)).astype(jnp.int32),
        ]
    )
    last = 2 * slots + 2 * count
    part = piece // CHUNKS
    outs = pl.pallas_call(
        functools.partial(select_kernel, slots, count, piece),
        grid_spec=pltpu.PrefetchScalarGridSpec(
            num_scalar_prefetch=1,
            grid=(slots + 1,),
            in_specs=[
                pl.BlockSpec(
                    (rows_block, block),
                    lambda s, t: (t[last], t[jnp.minimum(s, slots - 1)]),
                ),
                pl.BlockSpec(diag.shape, lambda s, t: (0, 0)),
            ]
            + [pl.BlockSpec(memory_space=pl.ANY)] * len(after),
            out_specs=[pl.BlockSpec((part, block), lambda s, t: (0, s))] * (count * CHUNKS),
        ),
        out_shape=[jax.ShapeDtypeStruct((part, (slots + 1) * block), F32)] * (count * CHUNKS),
        compiler_params=params(),
        cost_estimate=pl.CostEstimate(
            flops=0, transcendentals=0, bytes_accessed=8 * count * piece * (slots + 1) * block
        ),
        name="select",
    )(table, panel, diag, *after)
    return [outs[i * CHUNKS : (i + 1) * CHUNKS] for i in range(count)]


def assemble_kernel(leaf_parts, row_parts, piece, table, own_ref, *rest):
    parts, out_ref = rest[:-1], rest[-1]
    place, row = table[0], table[1]
    own_rows = own_ref.shape[0]
    out_ref[pl.ds(pl.multiple_of(place * own_rows, 8), own_rows), :] = own_ref[...]
    for k in range(row_parts):
        for d in range(1, leaf_parts):
            start = pl.multiple_of((place ^ d) * own_rows + (row ^ k) * piece, 8)
            out_ref[pl.ds(start, piece), :] = parts[k][pl.ds((d - 1) * piece, piece), :]


def assemble(own, parts, place, row):
    piece = own.shape[0] // len(parts)
    leaf_parts = own.shape[1] // own.shape[0]
    vmem = pl.BlockSpec(memory_space=pltpu.VMEM)
    return pl.pallas_call(
        functools.partial(assemble_kernel, leaf_parts, len(parts), piece),
        in_specs=[pl.BlockSpec(memory_space=pltpu.SMEM)] + [vmem] * (1 + len(parts)),
        out_specs=vmem,
        out_shape=jax.ShapeDtypeStruct((own.shape[1], own.shape[1]), F32),
        compiler_params=pltpu.CompilerParams(vmem_limit_bytes=VMEM_LIMIT),
        cost_estimate=pl.CostEstimate(
            flops=0, transcendentals=0, bytes_accessed=8 * own.shape[1] ** 2
        ),
        name="assemble",
    )(jnp.stack([place, row]).astype(jnp.int32), own, *parts)


def child_kernel(row_parts, table, cov_ref, *rest):
    parts = rest[:row_parts]
    out_ref, cov_h, cov_l, sel_h, sel_l, mid_h, mid_l, diag_s = rest[row_parts:]
    step = pl.program_id(0)
    row = table[0]
    piece = parts[0].shape[0]
    width = out_ref.shape[1]
    order = cov_ref.shape[0]

    @pl.when(step == 0)
    def _():
        for k in range(row_parts):
            away, u = divmod(k, CHUNKS)
            at = pl.ds(pl.multiple_of(((row ^ away) * CHUNKS + u) * piece, 16), piece)
            sel_h[at, :], sel_l[at, :] = split(parts[k][:, :order])
            diag_s[at, :] = parts[k][:, order:]
        for k in range(order // width):
            own = pl.ds(k * width, width)
            cov_h[own, :], cov_l[own, :] = split(cov_ref[own, :])

    cols = pl.ds(pl.multiple_of(step * width, 128), width)
    chosen = (sel_h[:, cols], sel_l[:, cols])
    for k in range(order // width):
        at = pl.ds(k * width, width)
        mid_h[at, :], mid_l[at, :] = split(dot3((cov_h[at, :], cov_l[at, :]), chosen, NN))
    product = (mid_h[...], mid_l[...])
    for k in range(order // width):
        at = pl.ds(k * width, width)
        out_ref[at, :] = dot3((sel_h[:, at], sel_l[:, at]), product, TN)
    out_ref[cols, :] += diag_s[cols, :]


def child_cov(cov, parts, row):
    order = cov.shape[0]
    row_parts = len(parts)
    block = parts[0].shape[1] - order
    whole = lambda shape: pl.BlockSpec(
        shape, lambda s, t: (0, 0), pipeline_mode=pl.Buffered(1)
    )
    return pl.pallas_call(
        functools.partial(child_kernel, row_parts),
        grid_spec=pltpu.PrefetchScalarGridSpec(
            num_scalar_prefetch=1,
            grid=(order // block,),
            in_specs=[whole(cov.shape)] + [whole(parts[0].shape)] * row_parts,
            out_specs=pl.BlockSpec((order, block), lambda s, t: (0, s)),
            scratch_shapes=[pltpu.VMEM((order, order), BF16)] * 4
            + [pltpu.VMEM((order, block), BF16)] * 2
            + [pltpu.VMEM((order, block), F32)],
        ),
        out_shape=jax.ShapeDtypeStruct((order, order), F32),
        compiler_params=params(),
        cost_estimate=pl.CostEstimate(
            flops=12 * order**3, transcendentals=0, bytes_accessed=12 * order**2
        ),
        name="child_cov",
    )(jnp.reshape(row, (1,)).astype(jnp.int32), cov, *parts)


def panel_kernel(cov_ref, panel_ref, diag_ref, cross_ref, marg_ref, cov_h, cov_l):
    order = cov_ref.shape[0]
    block = panel_ref.shape[1]

    @pl.when(pl.program_id(0) == 0)
    def _():
        for k in range(order // block):
            at = pl.ds(k * block, block)
            cov_h[at, :], cov_l[at, :] = split(cov_ref[at, :])

    cols = split(panel_ref[...])
    cross = -dot3((cov_h[...], cov_l[...]), cols, NN)
    cross_ref[...] = cross
    marg_ref[...] = diag_ref[...] - dot3(cols, split(cross), TN)


def level_panel(cov, panel, diag):
    order = cov.shape[0]
    block = diag.shape[1]
    count = panel.shape[1] // block
    return pl.pallas_call(
        panel_kernel,
        grid=(count,),
        in_specs=[
            pl.BlockSpec(cov.shape, lambda a: (0, 0), pipeline_mode=pl.Buffered(1)),
            pl.BlockSpec((order, block), lambda a: (0, a)),
            pl.BlockSpec((block, block), lambda a: (a, 0)),
        ],
        out_specs=[
            pl.BlockSpec((order, block), lambda a: (0, a)),
            pl.BlockSpec((block, block), lambda a: (a, 0)),
        ],
        out_shape=[
            jax.ShapeDtypeStruct(panel.shape, F32),
            jax.ShapeDtypeStruct(diag.shape, F32),
        ],
        scratch_shapes=[pltpu.VMEM((order, order), BF16)] * 2,
        compiler_params=params(),
        cost_estimate=pl.CostEstimate(
            flops=6 * panel.shape[1] * order * (order + block),
            transcendentals=0,
            bytes_accessed=4 * order * (order + 2 * panel.shape[1]),
        ),
        name="level_panel",
    )(cov, panel, diag)


def ownership(wanted, local_count, place):
    return wanted % local_count, wanted // local_count == place


def over_rows(mine):
    return over_core(mine, swap(mine, "rows", 2))


def over_core(mine, across):
    return [mine, swap(mine, "rows", 1), across, swap(across, "rows", 1)]


def by_distance(chunks):
    return [chunk[k] for k in range(len(chunks[0])) for chunk in chunks]


def local(
    sigma_top,
    panel_top,
    diag_top,
    panel_mid,
    diag_mid,
    pattern_mid,
    panel_low,
    diag_low,
    pattern_low,
):
    block = diag_top.shape[1]
    struct_rows = panel_top.shape[0]
    row_count = lax.axis_size("rows")
    leaf = lax.axis_index("leaf")
    row = lax.axis_index("rows")
    piece = struct_rows // row_count
    quad_place = leaf % 4
    quad_number = leaf // 4
    middle = leaf // 2
    mid_bit = middle % 2
    low_bit = leaf % 2

    top_local = panel_top.shape[1] // block

    def top_part(child, after):
        wanted, owned = ownership(pattern_mid[child], top_local, quad_place)
        zero = jnp.zeros_like(row)
        return select(
            panel_top, diag_top, wanted, owned, [zero], [row], row, piece, piece, after
        )[0]

    other_top = top_part(2 * quad_number + 1 - mid_bit, [])
    own_top = top_part(middle, other_top[:1])
    share = sigma_top.shape[0] // row_count
    sig = lax.dynamic_slice_in_dim(sigma_top, row * share, share, 0)
    sig_1 = swap(sig, "leaf", 1)
    sig_2 = swap(sig, "leaf", 2)
    sig_3 = swap(sig_1, "leaf", 2)
    top_selected = own_top[:1]
    own_top = [own + swap(other, "leaf", 2) for own, other in zip(own_top, other_top)]
    own_top = [own + swap(own, "leaf", 1) for own in own_top]
    sig_parts = over_rows(jnp.concatenate([sig_1, sig_2, sig_3], axis=0))

    mid_local = panel_mid.shape[1] // block
    places = [row ^ k for k in range(row_count)]

    def mid_part(child, after):
        wanted, owned = ownership(pattern_low[child], mid_local, low_bit * row_count + row)
        return select(
            panel_mid,
            diag_mid,
            wanted,
            owned,
            places,
            places,
            jnp.zeros_like(row),
            struct_rows,
            piece,
            after,
        )

    theirs = mid_part(2 * middle + 1 - low_bit, top_selected)
    ours = mid_part(leaf, theirs[0][:1])
    pairs = []
    for u in range(CHUNKS):
        far = theirs[2][u] + swap(theirs[3][u], "rows", 1)
        near = theirs[0][u] + swap(theirs[1][u], "rows", 1)
        own_far = ours[2][u] + swap(ours[3][u], "rows", 1)
        own_near = ours[0][u] + swap(ours[1][u], "rows", 1)
        pairs.append((far, near, own_far, own_near))
    pairs, own_top = lax.optimization_barrier((pairs, own_top))
    top_parts = by_distance([over_rows(own) for own in own_top])
    ours_far, ours_near = [], []
    for far, near, own_far, own_near in pairs:
        ours_far.append(own_far + swap(far, "leaf", 1))
        ours_near.append(own_near + swap(near, "leaf", 1))

    top_cov = assemble(sigma_top, sig_parts, quad_place, row)
    mid_cov = child_cov(top_cov, top_parts, row)
    sums = [ours_near[0] + swap(ours_far[0], "rows", 2)]
    across = [swap(sums[0], "rows", 2)]
    ours_far, mid_cov = lax.optimization_barrier((ours_far, mid_cov))
    for u in range(1, CHUNKS):
        sums.append(ours_near[u] + swap(ours_far[u], "rows", 2))
        across.append(swap(sums[u], "rows", 2))
    cross_mid, marginal_mid = level_panel(mid_cov, panel_mid, diag_mid)
    across, cross_mid, marginal_mid = lax.optimization_barrier((across, cross_mid, marginal_mid))
    mid_parts = by_distance([over_core(a, b) for a, b in zip(sums, across)])

    dot = functools.partial(jnp.dot, precision=HIGH, preferred_element_type=F32)
    cov_rows = lax.dynamic_slice_in_dim(top_cov, row * piece, piece, 0)
    cross_top = -dot(cov_rows, panel_top)
    own_rows = diag_top.shape[0] // row_count
    chunk = block if own_rows % block == 0 else own_rows - own_rows // block * block
    own_cols = lax.dynamic_slice_in_dim(panel_top, row * own_rows, own_rows, 1)
    product = dot(top_cov, own_cols)
    terms = []
    for i in range(own_rows // chunk):
        start = (row * own_rows + i * chunk) // block * block
        cols = lax.dynamic_slice_in_dim(panel_top, start, block, 1)
        terms.append(dot(product[:, i * chunk : (i + 1) * chunk].T, cols))
    own_diag = lax.dynamic_slice_in_dim(diag_top, row * own_rows, own_rows, 0)
    marginal_top = own_diag + jnp.concatenate(terms, axis=0)

    low_cov = child_cov(mid_cov, mid_parts, row)
    cross_low, marginal_low = level_panel(low_cov, panel_low, diag_low)
    return (cross_top, marginal_top, cross_mid, marginal_mid, cross_low, marginal_low)


def solution(mesh):
    return jax.shard_map(
        local,
        mesh=mesh,
        in_specs=(
            P("leaf", None),
            P(None, "leaf"),
            P("leaf", None),
            P(None, ("leaf", "rows")),
            P(("leaf", "rows"), None),
            P(),
            P(None, ("leaf", "rows")),
            P(("leaf", "rows"), None),
            P(),
        ),
        out_specs=(
            P("rows", "leaf"),
            P(("leaf", "rows"), None),
            P(None, ("leaf", "rows")),
            P(("leaf", "rows"), None),
            P(None, ("leaf", "rows")),
            P(("leaf", "rows"), None),
        ),
        check_vma=False,
    )
```
